32 devices in a mesh: island: 8 (over z, x), mp: 4 (over y, core).
Axes of the slice: x: 2, y: 2, z: 4, core: 2. Of those that a mesh axis runs over, the one named last changes fastest.
Arguments:
- acts: bfloat16 [8, 1024, 8192], P('island', None, 'mp'), may hold values from -6 to 6
- queries: bfloat16 [8, 1024, 4096], P('island', None, 'mp'), may hold values from -41 to 41
- keys_values: bfloat16 [8, 1024, 1024], P('island', 'mp'), may hold values from -4 to 4
- out_grad: bfloat16 [8, 1024, 4096], P('island', None, 'mp'), may hold values from -6 to 6
- segments: int32 [8, 1024], P('island'), may hold values from 0 to 15, never falling along the last dimension, each value on 1 to 512 neighbouring positions
- drift: bfloat16 [8, 8192, 1024], P('island', 'mp'), may hold values from -1.1953125 to 1.1953125
- outer_weights: float32 [4, 2048, 1024], P('mp', 'island'), may hold values from -6 to 6
- momentum: float32 [4, 2048, 1024], P('mp', 'island'), may hold values from -1.2 to 1.2
Outputs:
- query_grads: bfloat16 [8, 1024, 4096], P('island', None, 'mp')
- new_outer: float32 [4, 2048, 1024], P('mp', 'island')
- new_momentum: float32 [4, 2048, 1024], P('mp', 'island')
- next_weights: bfloat16 [4, 2048, 1024], P('mp')
The draws below stay inside these ranges and needn't reach their ends.
Inputs may be any that keep to these rules, and one draw needn't show every extreme that they name: `segments`: document ids never fall along a sequence.
All inputs are finite; a program needn't handle non-finite values.
Results may differ from the reference program's by a relative error of at most 0.0085.
Values may be sent and summed in bfloat16 or wider, within the bound.
No kernel may reach another device: no remote copies, remote signals or barrier semaphores. Data moves between devices by JAX's collectives and lax.ppermute only.
A program may use at most 192 MiB of HBM per device.

```python
import math
import jax
import jax.numpy as jnp
import numpy as np
from jax import lax

D = 8192
HD = 128
QH = 32
KVH = 4
TOK = 1024
KVW = 1024
ROWS_MP = 2048
ISLANDS = 8


def joint_draw(key):
    key_query = jax.random.fold_in(key, 101)
    key_keys = jax.random.fold_in(key, 102)
    key_values = jax.random.fold_in(key, 103)
    query_shape = (ISLANDS, TOK, QH * HD)
    head_shape = (ISLANDS, TOK, KVH * HD)
    queries = jax.random.truncated_normal(key_query, -4.0, 4.0, query_shape, jnp.float32)
    key_rows = jax.random.truncated_normal(key_keys, -4.0, 4.0, head_shape, jnp.float32)
    values = jax.random.truncated_normal(key_values, -4.0, 4.0, head_shape, jnp.float32)
    return (queries, jnp.concatenate([key_rows, values], axis=2))


def draw_queries(key, part):
    return joint_draw(key)[0].astype(jnp.bfloat16)


def draw_keys_values(key, part):
    return joint_draw(key)[1].astype(jnp.bfloat16)


def block_scale(key, extent, split, low, high):
    factor_of = 1.0
    for axis_at, blocks in split:
        steps = jax.random.uniform(jax.random.fold_in(jax.random.fold_in(key, 6), axis_at), (blocks,), jnp.float32, low / len(split), high / len(split))
        factor_of = factor_of * jnp.repeat(jnp.exp(steps), extent[axis_at] // blocks).reshape((-1,) + (1,) * (len(extent) - 1 - axis_at))
    return factor_of


def split_up(amount, total, most, skew):
    loads = [(1 << 20) // math.isqrt(grade ** skew) + 1 for grade in range(2, amount + 1)]
    rest, given = total - most - (amount - 1), [1] * (amount - 1)
    while rest > 0:
        candidates = [i for i in range(amount - 1) if given[i] < most]
        pool, budget = sum([loads[i] for i in candidates]), rest
        for i in candidates:
            extra = min(most - given[i], max(1, budget * loads[i] // pool), rest)
            given[i] = given[i] + extra
            rest = rest - extra
    return np.array([most] + given)


def ragged_sizes(stream_key, number_of, total, bound, lean):
    if number_of == 2:
        one = jax.random.randint(stream_key, (), max(1, total - bound), min(bound, total - 1) + 1)
        return jnp.stack([one, total - one])
    tallies = jnp.asarray(split_up(number_of, total, bound, lean), jnp.int32)
    couples = (number_of - 1) // 2
    source_of, receiver = tallies[1:1 + 2 * couples:2], tallies[2:2 + 2 * couples:2]
    slack = jnp.minimum(source_of - 1, bound - receiver)
    moved = jax.random.randint(jax.random.fold_in(stream_key, 1), (couples,), 0, 1 << 20) % (slack + 1)
    tallies = tallies.at[1:1 + 2 * couples:2].set(source_of - moved).at[2:2 + 2 * couples:2].set(receiver + moved)
    return tallies[jax.random.permutation(jax.random.fold_in(stream_key, 2), number_of)]


def gaussian(stream_key, extent, deviation, most, cuts=(), held_as=jnp.bfloat16):
    entries = deviation * jax.random.normal(stream_key, extent, jnp.float32)
    if cuts:
        entries = entries * block_scale(stream_key, extent, cuts, -0.22, 0.18)
    return jnp.clip(entries, -most, most).astype(held_as)


def setup_inputs(seed: int = 0) -> dict:
    seeds = jax.random.split(jax.random.key(seed), 9)
    acts = gaussian(seeds[0], (ISLANDS, TOK, D), 1.0, 6.0, ((0, 8), (2, 4)))
    queries = draw_queries(jax.random.fold_in(seeds[8], 71), 0)
    keys_values = draw_keys_values(jax.random.fold_in(seeds[8], 71), 0)
    out_grad = gaussian(seeds[3], (ISLANDS, TOK, QH * HD), 1.0, 6.0, ((0, 8), (2, 4)))
    segments = jax.vmap(lambda own: jnp.searchsorted(jnp.cumsum(ragged_sizes(own, max(4, TOK // 64), TOK, TOK // 2, 2)), jnp.arange(TOK), side="right"))(jax.random.split(seeds[4], ISLANDS)).reshape((ISLANDS, TOK)).astype(jnp.int32)
    drift = gaussian(seeds[5], (ISLANDS, D, KVW), 0.2, 1.1953125, ((0, 8), (1, 4)))
    outer_weights = gaussian(seeds[6], (D // ROWS_MP, ROWS_MP, KVW), 1.0, 6.0, ((0, 4), (1, 8)), jnp.float32)
    momentum = gaussian(seeds[7], (D // ROWS_MP, ROWS_MP, KVW), 0.2, 1.2, ((0, 4), (1, 8)), jnp.float32)
    return dict(acts=acts, queries=queries, keys_values=keys_values, out_grad=out_grad, segments=segments, drift=drift, outer_weights=outer_weights, momentum=momentum)


INNER_LR = 0.8
OUTER_LR = 0.7
MOMENTUM = 0.9
ROPE_BASE = 500000.0

def rope_tables(positions, head_width):
    half_width = head_width // 2
    exponent = jnp.arange(half_width, dtype=jnp.float32) * (2.0 / head_width)
    frequency = jnp.power(jnp.float32(ROPE_BASE), -exponent)
    angles = jnp.arange(positions, dtype=jnp.float32)[:, None] * frequency[None, :]
    return (jnp.cos(angles), jnp.sin(angles))

def unrotate(grads, cosine, sine_table):
    half_width = grads.shape[-1] // 2
    first_half = grads[..., :half_width]
    second_half = grads[..., half_width:]
    cos_wide = cosine[:, None, :]
    sin_wide = sine_table[:, None, :]
    return jnp.concatenate([first_half * cos_wide + second_half * sin_wide, second_half * cos_wide - first_half * sin_wide], axis=-1)

def island_step(running, operands):
    acts_rows, query_rows, kv_rows, grad_rows, segment_ids, drift_rows = operands
    score_scale = 1.0 / math.sqrt(HD)
    half_kv = KVH * HD
    queries_f = query_rows.reshape(TOK, QH, HD).astype(jnp.float32)
    keys_f = jnp.repeat(kv_rows[:, :half_kv].reshape(TOK, KVH, HD), QH // KVH, axis=1).astype(jnp.float32)
    values_f = jnp.repeat(kv_rows[:, half_kv:].reshape(TOK, KVH, HD), QH // KVH, axis=1).astype(jnp.float32)
    grads_f = grad_rows.reshape(TOK, QH, HD).astype(jnp.float32)
    positions = jnp.arange(TOK)
    allowed = (positions[:, None] >= positions[None, :]) & (segment_ids[:, None] == segment_ids[None, :])
    scores = jnp.einsum('qhd,khd->hqk', queries_f, keys_f) * score_scale
    scores = jnp.where(allowed[None], scores, -jnp.inf)
    shifted = scores - lax.optimization_barrier(jnp.max(scores, axis=-1, keepdims=True))
    weights = jnp.exp(shifted)
    attn_probs = weights / lax.optimization_barrier(jnp.sum(weights, axis=-1, keepdims=True))
    probs_low = lax.optimization_barrier(attn_probs.astype(jnp.bfloat16)).astype(jnp.float32)
    value_grads = jnp.einsum('hqk,qhd->khd', probs_low, grads_f)
    dprobs = jnp.einsum('qhd,khd->hqk', grads_f, values_f)
    row_dot = lax.optimization_barrier(jnp.sum(attn_probs * dprobs, axis=-1, keepdims=True))
    dscores = lax.optimization_barrier((attn_probs * (dprobs - row_dot)).astype(jnp.bfloat16)).astype(jnp.float32)
    query_grads = (jnp.einsum('hqk,khd->qhd', dscores, keys_f) * score_scale).astype(jnp.bfloat16)
    key_grads = jnp.einsum('hqk,qhd->khd', dscores, queries_f) * score_scale
    key_sum = lax.optimization_barrier(jnp.sum(key_grads.reshape(TOK, KVH, QH // KVH, HD), axis=2))
    value_sum = lax.optimization_barrier(jnp.sum(value_grads.reshape(TOK, KVH, QH // KVH, HD), axis=2))
    cosine, sine_table = rope_tables(TOK, HD)
    key_plain = unrotate(key_sum, cosine, sine_table)
    grads_low = jnp.concatenate([key_plain.reshape(TOK, half_kv), value_sum.reshape(TOK, half_kv)], axis=1).astype(jnp.bfloat16)
    weight_grads = jnp.dot(acts_rows.T, grads_low, preferred_element_type=jnp.float32) * (1.0 / math.sqrt(D))
    new_drift = drift_rows.astype(jnp.float32) - INNER_LR * weight_grads
    return (running + new_drift, query_grads.reshape(TOK, QH * HD))

def reference(acts, queries, keys_values, out_grad, segments, drift, outer_weights, momentum):
    start = jnp.zeros((D, KVW), jnp.float32)
    drift_sum, query_grads = lax.scan(island_step, start, (acts, queries, keys_values, out_grad, segments, drift))
    outer_grad = -(drift_sum / ISLANDS)
    outer_grad = outer_grad.reshape(D // ROWS_MP, ROWS_MP, KVW)
    new_momentum = MOMENTUM * momentum + outer_grad
    new_outer = outer_weights - OUTER_LR * (outer_grad + MOMENTUM * new_momentum)
    return (query_grads, new_outer, new_momentum, new_outer.astype(jnp.bfloat16))
```

```python
import functools
import math

import jax
import jax.numpy as jnp
from jax import lax
from jax.experimental import pallas as pl
from jax.experimental.pallas import tpu as pltpu
from jax.sharding import PartitionSpec as P

D = 8192
HD = 128
QH = 32
KVH = 4

INNER_LR = 0.8
OUTER_LR = 0.7
MOMENTUM = 0.9
ROPE_BASE = 500000.0

TB = 128
UB = 128
NEG = -1e30
LOG2E = 1.4426950408889634
MIB = 1 << 20


def dot_nt(a, b):
    return lax.dot_general(a, b, (((1,), (1,)), ((), ())), preferred_element_type=jnp.float32)


def dot_nn(a, b):
    return lax.dot_general(a, b, (((1,), (0,)), ((), ())), preferred_element_type=jnp.float32)


def rope_tables(positions, head_width):
    half_width = head_width // 2
    exponent = jnp.arange(half_width, dtype=jnp.float32) * (2.0 / head_width)
    frequency = jnp.power(jnp.float32(ROPE_BASE), -exponent)
    angles = jnp.arange(positions, dtype=jnp.float32)[:, None] * frequency[None, :]
    return (jnp.cos(angles), jnp.sin(angles))


def stack_heads(block, heads):
    return jnp.concatenate([block[:, h * HD : (h + 1) * HD] for h in range(heads)], axis=0)


def block_mask(start_row, t_base, u_base):
    u_at = lax.broadcasted_iota(jnp.int32, (UB, TB), 0) + u_base
    t_at = lax.broadcasted_iota(jnp.int32, (UB, TB), 1) + t_base
    return (u_at <= t_at) & (u_at >= start_row)


def fold_rows(x, op):
    parts = [x[i * 8 : (i + 1) * 8] for i in range(x.shape[0] // 8)]
    while len(parts) > 1:
        parts = [op(parts[i], parts[i + 1]) if i + 1 < len(parts) else parts[i] for i in range(0, len(parts), 2)]
    return parts[0]


def value_kernel(low_ref, start_ref, q_ref, g_ref, k_ref, dv_ref, top_ref, inv_ref, s_scr, acc_scr, qc_scr, gc_scr, *, heads, scale2):
    tb = pl.program_id(0)
    width = heads * TB
    low = low_ref[tb]
    high = (tb * TB + TB - 1) // UB + 1

    @pl.when(tb == 0)
    def _():
        acc_scr[...] = jnp.zeros_like(acc_scr)

    for h in range(heads):
        qc_scr[h * TB : (h + 1) * TB, :] = q_ref[:, h * HD : (h + 1) * HD]
        gc_scr[h * TB : (h + 1) * TB, :] = g_ref[:, h * HD : (h + 1) * HD]
    start_row = start_ref[...]

    def scores(ub, top):
        u_base = pl.multiple_of(ub * UB, UB)
        mask = block_mask(start_row, tb * TB, u_base)
        raw = dot_nt(k_ref[pl.ds(u_base, UB), :], qc_scr[...])
        tops = []
        for h in range(heads):
            s = jnp.where(mask, raw[:, h * TB : (h + 1) * TB] * scale2, NEG)
            s_scr[pl.ds(u_base, UB), h * TB : (h + 1) * TB] = s
            tops.append(fold_rows(s, jnp.maximum))
        return jnp.maximum(top, jnp.concatenate(tops, axis=1))

    top8 = lax.fori_loop(low, high, scores, jnp.full((8, width), NEG, jnp.float32))
    top = jnp.max(top8, axis=0, keepdims=True)
    top_ref[0] = top

    def weights(ub, total):
        u_base = pl.multiple_of(ub * UB, UB)
        p = jnp.exp2(s_scr[pl.ds(u_base, UB), :] - top)
        s_scr[pl.ds(u_base, UB), :] = p
        return total + fold_rows(p, jnp.add)

    total8 = lax.fori_loop(low, high, weights, jnp.zeros((8, width), jnp.float32))
    inv = 1.0 / jnp.sum(total8, axis=0, keepdims=True)
    inv_ref[0] = inv

    def grads(ub, carry):
        u_base = pl.multiple_of(ub * UB, UB)
        p = (s_scr[pl.ds(u_base, UB), :] * inv).astype(jnp.bfloat16)
        acc_scr[pl.ds(u_base, UB), :] += dot_nn(p, gc_scr[...])
        return carry

    lax.fori_loop(low, high, grads, 0)

    @pl.when(tb == pl.num_programs(0) - 1)
    def _():
        dv_ref[...] = acc_scr[...].astype(dv_ref.dtype)


def key_kernel(
    low_ref, start_ref, q_ref, g_ref, k_ref, kt_ref, v_ref, top_ref, inv_ref, cos_ref, sin_ref, dk_ref, dq_ref,
    p_scr, d_scr, acc_scr, qc_scr, gc_scr, dqt_scr, *, heads, scale2, scale
):
    tb = pl.program_id(0)
    width = heads * TB
    low = low_ref[tb]
    high = (tb * TB + TB - 1) // UB + 1

    @pl.when(tb == 0)
    def _():
        acc_scr[...] = jnp.zeros_like(acc_scr)

    for h in range(heads):
        qc_scr[h * TB : (h + 1) * TB, :] = q_ref[:, h * HD : (h + 1) * HD]
        gc_scr[h * TB : (h + 1) * TB, :] = g_ref[:, h * HD : (h + 1) * HD]
    start_row = start_ref[...]
    top = top_ref[0]
    inv = inv_ref[0]

    def first(ub, total):
        u_base = pl.multiple_of(ub * UB, UB)
        mask = block_mask(start_row, tb * TB, u_base)
        raw = dot_nt(k_ref[pl.ds(u_base, UB), :], qc_scr[...])
        dp = dot_nt(v_ref[pl.ds(u_base, UB), :], gc_scr[...])
        sums = []
        for h in range(heads):
            cols = slice(h * TB, (h + 1) * TB)
            s = jnp.where(mask, raw[:, cols] * scale2, NEG)
            p = jnp.exp2(s - top[:, cols]) * inv[:, cols]
            p_scr[pl.ds(u_base, UB), cols] = p
            d_scr[pl.ds(u_base, UB), cols] = dp[:, cols]
            sums.append(fold_rows(p * dp[:, cols], jnp.add))
        return total + jnp.concatenate(sums, axis=1)

    total8 = lax.fori_loop(low, high, first, jnp.zeros((8, width), jnp.float32))
    row_dot = jnp.sum(total8, axis=0, keepdims=True)
    dqt_scr[...] = jnp.zeros_like(dqt_scr)

    def second(ub, carry):
        u_base = pl.multiple_of(ub * UB, UB)
        ds = (p_scr[pl.ds(u_base, UB), :] * (d_scr[pl.ds(u_base, UB), :] - row_dot)).astype(jnp.bfloat16)
        acc_scr[pl.ds(u_base, UB), :] += dot_nn(ds, qc_scr[...])
        dqt_scr[...] += dot_nn(kt_ref[:, pl.ds(u_base, UB)], ds)
        return carry

    lax.fori_loop(low, high, second, 0)
    for h in range(heads):
        dq_ref[:, h * HD : (h + 1) * HD] = (dqt_scr[:, h * TB : (h + 1) * TB].T * scale).astype(dq_ref.dtype)

    @pl.when(tb == pl.num_programs(0) - 1)
    def _():
        dk = acc_scr[...] * scale
        dk_ref[...] = (dk * cos_ref[...] + pltpu.roll(dk, HD // 2, 1) * sin_ref[...]).astype(dk_ref.dtype)


def attention_values(low, start, q, g, k, out_dtype):
    tok, cols = q.shape
    heads = cols // HD
    steps = tok // TB
    scale2 = LOG2E / math.sqrt(HD)
    width = heads * TB
    return pl.pallas_call(
        functools.partial(value_kernel, heads=heads, scale2=scale2),
        grid_spec=pltpu.PrefetchScalarGridSpec(
            num_scalar_prefetch=1,
            grid=(steps,),
            in_specs=[
                pl.BlockSpec((1, TB), lambda i, lo: (0, i)),
                pl.BlockSpec((TB, cols), lambda i, lo: (i, 0)),
                pl.BlockSpec((TB, cols), lambda i, lo: (i, 0)),
                pl.BlockSpec((tok, HD), lambda i, lo: (0, 0)),
            ],
            out_specs=[
                pl.BlockSpec((tok, HD), lambda i, lo: (0, 0)),
                pl.BlockSpec((1, 1, width), lambda i, lo: (i, 0, 0)),
                pl.BlockSpec((1, 1, width), lambda i, lo: (i, 0, 0)),
            ],
            scratch_shapes=[
                pltpu.VMEM((tok, width), jnp.float32),
                pltpu.VMEM((tok, HD), jnp.float32),
                pltpu.VMEM((width, HD), jnp.bfloat16),
                pltpu.VMEM((width, HD), jnp.bfloat16),
            ],
        ),
        out_shape=[
            jax.ShapeDtypeStruct((tok, HD), out_dtype),
            jax.ShapeDtypeStruct((steps, 1, width), jnp.float32),
            jax.ShapeDtypeStruct((steps, 1, width), jnp.float32),
        ],
        cost_estimate=pl.CostEstimate(flops=4 * 18 * UB * width * HD, bytes_accessed=2 * tok * cols * 2, transcendentals=0),
        compiler_params=pltpu.CompilerParams(dimension_semantics=("arbitrary",), vmem_limit_bytes=40 * MIB),
        name="value_grads",
    )(low, start, q, g, k)


def attention_keys(low, start, q, g, k, v, top, inv, cos_wide, sin_wide, out_dtype):
    tok, cols = q.shape
    heads = cols // HD
    steps = tok // TB
    width = heads * TB
    return pl.pallas_call(
        functools.partial(key_kernel, heads=heads, scale2=LOG2E / math.sqrt(HD), scale=1.0 / math.sqrt(HD)),
        grid_spec=pltpu.PrefetchScalarGridSpec(
            num_scalar_prefetch=1,
            grid=(steps,),
            in_specs=[
                pl.BlockSpec((1, TB), lambda i, lo: (0, i)),
                pl.BlockSpec((TB, cols), lambda i, lo: (i, 0)),
                pl.BlockSpec((TB, cols), lambda i, lo: (i, 0)),
                pl.BlockSpec((tok, HD), lambda i, lo: (0, 0)),
                pl.BlockSpec((HD, tok), lambda i, lo: (0, 0)),
                pl.BlockSpec((tok, HD), lambda i, lo: (0, 0)),
                pl.BlockSpec((1, 1, width), lambda i, lo: (i, 0, 0)),
                pl.BlockSpec((1, 1, width), lambda i, lo: (i, 0, 0)),
                pl.BlockSpec((tok, HD), lambda i, lo: (0, 0)),
                pl.BlockSpec((tok, HD), lambda i, lo: (0, 0)),
            ],
            out_specs=[
                pl.BlockSpec((tok, HD), lambda i, lo: (0, 0)),
                pl.BlockSpec((TB, cols), lambda i, lo: (i, 0)),
            ],
            scratch_shapes=[
                pltpu.VMEM((tok, width), jnp.float32),
                pltpu.VMEM((tok, width), jnp.float32),
                pltpu.VMEM((tok, HD), jnp.float32),
                pltpu.VMEM((width, HD), jnp.bfloat16),
                pltpu.VMEM((width, HD), jnp.bfloat16),
                pltpu.VMEM((HD, width), jnp.float32),
            ],
        ),
        out_shape=[
            jax.ShapeDtypeStruct((tok, HD), out_dtype),
            jax.ShapeDtypeStruct((tok, cols), jnp.bfloat16),
        ],
        cost_estimate=pl.CostEstimate(flops=8 * 18 * UB * width * HD, bytes_accessed=3 * tok * cols * 2, transcendentals=0),
        compiler_params=pltpu.CompilerParams(dimension_semantics=("arbitrary",), vmem_limit_bytes=40 * MIB),
        name="key_grads",
    )(low, start, q, g, k, k.T, v, top, inv, cos_wide, sin_wide)


def partial_kernel(order_ref, a_ref, g_ref, drift_ref, out_ref, *, factor):
    grad = dot_nn(a_ref[...], g_ref[...])
    out_ref[0] = (drift_ref[...].astype(jnp.float32) - factor * grad).astype(out_ref.dtype)


def island_partials(orders, acts_t, grads, drift, column, factor):
    rows, tok = acts_t.shape
    width = grads.shape[1]
    count = orders.shape[0] // 2
    block = rows // count
    part = width // 2
    out_cols = drift.shape[1] // part
    base = column // part
    return pl.pallas_call(
        functools.partial(partial_kernel, factor=factor),
        grid_spec=pltpu.PrefetchScalarGridSpec(
            num_scalar_prefetch=1,
            grid=(count, 2),
            in_specs=[
                pl.BlockSpec((block, tok), lambda s, d, o: (o[2 * s + d], 0)),
                pl.BlockSpec((tok, part), lambda s, d, o: (0, d)),
                pl.BlockSpec((block, part), lambda s, d, o: (o[2 * s + d], base + d)),
            ],
            out_specs=pl.BlockSpec((1, block, part), lambda s, d, o: (2 * s + d, 0, 0)),
        ),
        out_shape=jax.ShapeDtypeStruct((2 * count, block, part), jnp.bfloat16),
        cost_estimate=pl.CostEstimate(
            flops=2 * rows * tok * width, bytes_accessed=2 * (rows * tok + tok * width + 2 * rows * width), transcendentals=0
        ),
        compiler_params=pltpu.CompilerParams(dimension_semantics=("arbitrary", "arbitrary"), vmem_limit_bytes=32 * MIB),
        name="partials",
    )(orders, acts_t, grads, drift)


def ring_order(count):
    return [i for i in range(0, count, 2)] + [i for i in reversed(range(1, count, 2))]


def ring_tables(count):
    ring = ring_order(count)
    place = [ring.index(i) for i in range(count)]
    up, down = [], []
    for i in range(count):
        up.append([ring[(place[i] - 1 - s) % count] for s in range(count)])
        down.append([ring[(place[i] + 1 + s) % count] for s in range(count)])
    ups = [(ring[i], ring[(i + 1) % count]) for i in range(count)]
    downs = [(ring[i], ring[(i - 1) % count]) for i in range(count)]
    return up, down, ups, downs


def ring_sum(parts, count, direction, perm):
    held = parts[direction]
    for step in range(1, count):
        held = lax.ppermute(held, "island", perm)
        own = parts[2 * step + direction]
        held = held.astype(jnp.float32) + own.astype(jnp.float32)
        if step < count - 1:
            held = held.astype(jnp.bfloat16)
    return held


def fetch_heads(keys_values, mp_count, local_heads):
    half = keys_values.shape[1] // 2
    rows = keys_values.shape[0]
    group = QH // KVH
    me = lax.axis_index("mp")

    def pick(device):
        head = device * local_heads // group
        return jnp.concatenate(
            [
                lax.dynamic_slice_in_dim(keys_values, head * HD, HD, 1),
                lax.dynamic_slice_in_dim(keys_values, half + head * HD, HD, 1),
            ],
            axis=1,
        )

    if mp_count & (mp_count - 1) or mp_count > 4:
        stacked = jnp.stack([pick(j) for j in range(mp_count)])
        return lax.all_to_all(stacked, "mp", split_axis=0, concat_axis=0, tiled=True).reshape(mp_count * rows, 2 * HD)
    whole = jnp.zeros((mp_count, rows, 2 * HD), keys_values.dtype)
    got = [pick(me)] + [
        lax.ppermute(pick(me ^ k), "mp", [(i, i ^ k) for i in range(mp_count)]) for k in range(1, mp_count)
    ]
    for k in range(mp_count):
        whole = lax.dynamic_update_index_in_dim(whole, got[k], me ^ k, 0)
    return whole.reshape(mp_count * rows, 2 * HD)


def gather_columns(piece, mp_count):
    if mp_count != 4:
        return lax.all_gather(piece, "mp", axis=1, tiled=True)
    me = lax.axis_index("mp")
    far = lax.ppermute(piece, "mp", [(i, i ^ 2) for i in range(mp_count)])
    near = lax.ppermute(piece, "mp", [(i, i ^ 1) for i in range(mp_count)])
    far_near = lax.ppermute(far, "mp", [(i, i ^ 1) for i in range(mp_count)])
    odd = (me & 1) == 1
    upper = (me & 2) == 2
    mine = jnp.where(odd, jnp.concatenate([near, piece], 1), jnp.concatenate([piece, near], 1))
    other = jnp.where(odd, jnp.concatenate([far_near, far], 1), jnp.concatenate([far, far_near], 1))
    return jnp.where(upper, jnp.concatenate([other, mine], 1), jnp.concatenate([mine, other], 1))


def fold_and_gather(piece, mp_count):
    tok = piece.shape[0]
    rows = tok // mp_count
    received = lax.all_to_all(piece.astype(jnp.bfloat16), "mp", split_axis=0, concat_axis=0, tiled=True)
    received = received.astype(jnp.float32).reshape(KVH, mp_count // KVH, rows, HD)
    block = jnp.transpose(jnp.sum(received, axis=1), (1, 0, 2)).reshape(rows, KVH * HD)
    return lax.all_gather(block.astype(jnp.bfloat16), "mp", axis=0, tiled=True)


def body(acts, queries, keys_values, out_grad, segments, drift, outer_weights, momentum):
    tok = acts.shape[1]
    island_count = lax.axis_size("island")
    mp_count = lax.axis_size("mp")
    local_heads = queries.shape[2] // HD
    whole_groups = mp_count == KVH
    pair = fetch_heads(keys_values[0], mp_count, local_heads)
    keys, values = pair[:, :HD], pair[:, HD:]
    ids = segments[0]
    start = jnp.sum((ids[None, :] < ids[:, None]).astype(jnp.int32), axis=1)
    low = start[::TB] // UB
    start = start[None, :]
    cosine, sine = rope_tables(tok, HD)
    cos_wide = jnp.concatenate([cosine, cosine], axis=1)
    sin_wide = jnp.concatenate([sine, -sine], axis=1)
    acts_t = acts[0].T
    up, down, ups, downs = ring_tables(island_count)
    me = lax.axis_index("island")
    orders = jnp.stack([jnp.array(up, jnp.int32)[me], jnp.array(down, jnp.int32)[me]], axis=1).reshape(-1)
    factor = INNER_LR / math.sqrt(D)

    piece_type = jnp.bfloat16 if whole_groups else jnp.float32
    q, g = queries[0], out_grad[0]
    value_piece, top, inv = attention_values(low, start, q, g, keys, piece_type)
    gather = gather_columns if whole_groups else fold_and_gather
    value_low = gather(value_piece, mp_count)
    key_piece, query_grads = attention_keys(low, start, q, g, keys, values, top, inv, cos_wide, sin_wide, piece_type)
    half = keys_values.shape[2] // 2
    value_parts = island_partials(orders, acts_t, value_low, drift[0], half, factor)
    key_low = gather(key_piece, mp_count)
    key_parts = island_partials(orders, acts_t, key_low, drift[0], 0, factor)
    columns = []
    for parts in (value_parts, key_parts):
        columns.append([ring_sum(parts, island_count, d, (ups, downs)[d]) for d in range(2)])
    order = [columns[1][0], columns[1][1], columns[0][0], columns[0][1]]
    part = half // 2
    outer, moment, blocks = [], [], []
    for i, total in enumerate(order):
        cols = slice(i * part, (i + 1) * part)
        outer_grad = -(total / island_count)
        new_momentum = MOMENTUM * momentum[0, :, cols] + outer_grad
        new_outer = outer_weights[0, :, cols] - OUTER_LR * (outer_grad + MOMENTUM * new_momentum)
        outer.append(new_outer)
        moment.append(new_momentum)
        blocks.append(new_outer.astype(jnp.bfloat16))
    rows = blocks[0].shape[0]
    gathered = jnp.zeros((island_count, rows, 2 * half), jnp.bfloat16)
    for i in (2, 3, 0, 1):
        held = blocks[i]
        table = (up, down)[i % 2]
        perm = (ups, downs)[i % 2]
        gathered = lax.dynamic_update_slice(gathered, held[None], (me, 0, i * part))
        for step in range(island_count - 1):
            held = lax.ppermute(held, "island", perm)
            owner = orders[2 * step + i % 2]
            gathered = lax.dynamic_update_slice(gathered, held[None], (owner, 0, i * part))
    new_outer = jnp.concatenate(outer, axis=1)
    new_momentum = jnp.concatenate(moment, axis=1)
    next_weights = gathered.reshape(island_count * rows, 2 * half)
    return (query_grads[None], new_outer[None], new_momentum[None], next_weights[None])


def solution(mesh):
    in_specs = (
        P("island", None, "mp"),
        P("island", None, "mp"),
        P("island", "mp", None),
        P("island", None, "mp"),
        P("island", None),
        P("island", "mp", None),
        P("mp", "island", None),
        P("mp", "island", None),
    )
    out_specs = (
        P("island", None, "mp"),
        P("mp", "island", None),
        P("mp", "island", None),
        P("mp", None, None),
    )
    return jax.shard_map(body, mesh=mesh, in_specs=in_specs, out_specs=out_specs, check_vma=False)
```

```python
import functools
import math

import jax
import jax.numpy as jnp
from jax import lax
from jax.experimental import pallas as pl
from jax.experimental.pallas import tpu as pltpu
from jax.sharding import PartitionSpec as P

D = 8192
HD = 128
QH = 32
KVH = 4

INNER_LR = 0.8
OUTER_LR = 0.7
MOMENTUM = 0.9
ROPE_BASE = 500000.0

TB = 128
UB = 128
NEG = -1e30
LOG2E = 1.4426950408889634
VMEM_LIMIT = 60 << 20


def dot_nt(a, b):
    return lax.dot_general(a, b, (((1,), (1,)), ((), ())), preferred_element_type=jnp.float32)


def dot_nn(a, b):
    return lax.dot_general(a, b, (((1,), (0,)), ((), ())), preferred_element_type=jnp.float32)


def rope_tables(positions, head_width):
    half_width = head_width // 2
    exponent = jnp.arange(half_width, dtype=jnp.float32) * (2.0 / head_width)
    frequency = jnp.power(jnp.float32(ROPE_BASE), -exponent)
    angles = jnp.arange(positions, dtype=jnp.float32)[:, None] * frequency[None, :]
    return (jnp.cos(angles), jnp.sin(angles))


def stack_heads(block, heads):
    return jnp.concatenate([block[:, h * HD : (h + 1) * HD] for h in range(heads)], axis=0)


def block_mask(start_row, t_base, u_base):
    u_at = lax.broadcasted_iota(jnp.int32, (UB, TB), 0) + u_base
    t_at = lax.broadcasted_iota(jnp.int32, (UB, TB), 1) + t_base
    return (u_at <= t_at) & (u_at >= start_row)


def fold_rows(x, op):
    parts = [x[i * 8 : (i + 1) * 8] for i in range(x.shape[0] // 8)]
    while len(parts) > 1:
        parts = [op(parts[i], parts[i + 1]) if i + 1 < len(parts) else parts[i] for i in range(0, len(parts), 2)]
    return parts[0]


def value_kernel(low_ref, start_ref, q_ref, g_ref, k_ref, dv_ref, top_ref, inv_ref, s_scr, acc_scr, qc_scr, gc_scr, *, heads, scale2):
    tb = pl.program_id(0)
    width = heads * TB
    low = low_ref[tb]
    high = (tb * TB + TB - 1) // UB + 1

    @pl.when(tb == 0)
    def _():
        acc_scr[...] = jnp.zeros_like(acc_scr)

    for h in range(heads):
        qc_scr[h * TB : (h + 1) * TB, :] = q_ref[:, h * HD : (h + 1) * HD]
        gc_scr[h * TB : (h + 1) * TB, :] = g_ref[:, h * HD : (h + 1) * HD]
    start_row = start_ref[...]

    def scores(ub, top):
        u_base = pl.multiple_of(ub * UB, UB)
        mask = block_mask(start_row, tb * TB, u_base)
        raw = dot_nt(k_ref[pl.ds(u_base, UB), :], qc_scr[...])
        tops = []
        for h in range(heads):
            s = jnp.where(mask, raw[:, h * TB : (h + 1) * TB] * scale2, NEG)
            s_scr[pl.ds(u_base, UB), h * TB : (h + 1) * TB] = s
            tops.append(fold_rows(s, jnp.maximum))
        return jnp.maximum(top, jnp.concatenate(tops, axis=1))

    top8 = lax.fori_loop(low, high, scores, jnp.full((8, width), NEG, jnp.float32))
    top = jnp.max(top8, axis=0, keepdims=True)
    top_ref[0] = top

    def weights(ub, total):
        u_base = pl.multiple_of(ub * UB, UB)
        p = jnp.exp2(s_scr[pl.ds(u_base, UB), :] - top)
        s_scr[pl.ds(u_base, UB), :] = p
        return total + fold_rows(p, jnp.add)

    total8 = lax.fori_loop(low, high, weights, jnp.zeros((8, width), jnp.float32))
    inv = 1.0 / jnp.sum(total8, axis=0, keepdims=True)
    inv_ref[0] = inv

    def grads(ub, carry):
        u_base = pl.multiple_of(ub * UB, UB)
        p = (s_scr[pl.ds(u_base, UB), :] * inv).astype(jnp.bfloat16)
        acc_scr[pl.ds(u_base, UB), :] += dot_nn(p, gc_scr[...])
        return carry

    lax.fori_loop(low, high, grads, 0)

    @pl.when(tb == pl.num_programs(0) - 1)
    def _():
        dv_ref[...] = acc_scr[...].astype(dv_ref.dtype)


def key_kernel(
    low_ref, start_ref, q_ref, g_ref, k_ref, kt_ref, v_ref, top_ref, inv_ref, cos_ref, sin_ref, dk_ref, dq_ref,
    p_scr, d_scr, acc_scr, qc_scr, gc_scr, dqt_scr, *, heads, scale2, scale
):
    tb = pl.program_id(0)
    width = heads * TB
    low = low_ref[tb]
    high = (tb * TB + TB - 1) // UB + 1

    @pl.when(tb == 0)
    def _():
        acc_scr[...] = jnp.zeros_like(acc_scr)

    for h in range(heads):
        qc_scr[h * TB : (h + 1) * TB, :] = q_ref[:, h * HD : (h + 1) * HD]
        gc_scr[h * TB : (h + 1) * TB, :] = g_ref[:, h * HD : (h + 1) * HD]
    start_row = start_ref[...]
    top = top_ref[0]
    inv = inv_ref[0]

    def first(ub, total):
        u_base = pl.multiple_of(ub * UB, UB)
        mask = block_mask(start_row, tb * TB, u_base)
        raw = dot_nt(k_ref[pl.ds(u_base, UB), :], qc_scr[...])
        dp = dot_nt(v_ref[pl.ds(u_base, UB), :], gc_scr[...])
        sums = []
        for h in range(heads):
            cols = slice(h * TB, (h + 1) * TB)
            s = jnp.where(mask, raw[:, cols] * scale2, NEG)
            p = jnp.exp2(s - top[:, cols]) * inv[:, cols]
            p_scr[pl.ds(u_base, UB), cols] = p
            d_scr[pl.ds(u_base, UB), cols] = dp[:, cols]
            sums.append(fold_rows(p * dp[:, cols], jnp.add))
        return total + jnp.concatenate(sums, axis=1)

    total8 = lax.fori_loop(low, high, first, jnp.zeros((8, width), jnp.float32))
    row_dot = jnp.sum(total8, axis=0, keepdims=True)
    dqt_scr[...] = jnp.zeros_like(dqt_scr)

    def second(ub, carry):
        u_base = pl.multiple_of(ub * UB, UB)
        ds = (p_scr[pl.ds(u_base, UB), :] * (d_scr[pl.ds(u_base, UB), :] - row_dot)).astype(jnp.bfloat16)
        acc_scr[pl.ds(u_base, UB), :] += dot_nn(ds, qc_scr[...])
        dqt_scr[...] += dot_nn(kt_ref[:, pl.ds(u_base, UB)], ds)
        return carry

    lax.fori_loop(low, high, second, 0)
    for h in range(heads):
        dq_ref[:, h * HD : (h + 1) * HD] = (dqt_scr[:, h * TB : (h + 1) * TB].T * scale).astype(dq_ref.dtype)

    @pl.when(tb == pl.num_programs(0) - 1)
    def _():
        dk = acc_scr[...] * scale
        dk_ref[...] = (dk * cos_ref[...] + pltpu.roll(dk, HD // 2, 1) * sin_ref[...]).astype(dk_ref.dtype)


def attention_values(low, start, q, g, k, out_dtype):
    tok, cols = q.shape
    heads = cols // HD
    steps = tok // TB
    scale2 = LOG2E / math.sqrt(HD)
    width = heads * TB
    return pl.pallas_call(
        functools.partial(value_kernel, heads=heads, scale2=scale2),
        grid_spec=pltpu.PrefetchScalarGridSpec(
            num_scalar_prefetch=1,
            grid=(steps,),
            in_specs=[
                pl.BlockSpec((1, TB), lambda i, lo: (0, i)),
                pl.BlockSpec((TB, cols), lambda i, lo: (i, 0)),
                pl.BlockSpec((TB, cols), lambda i, lo: (i, 0)),
                pl.BlockSpec((tok, HD), lambda i, lo: (0, 0)),
            ],
            out_specs=[
                pl.BlockSpec((tok, HD), lambda i, lo: (0, 0)),
                pl.BlockSpec((1, 1, width), lambda i, lo: (i, 0, 0)),
                pl.BlockSpec((1, 1, width), lambda i, lo: (i, 0, 0)),
            ],
            scratch_shapes=[
                pltpu.VMEM((tok, width), jnp.float32),
                pltpu.VMEM((tok, HD), jnp.float32),
                pltpu.VMEM((width, HD), jnp.bfloat16),
                pltpu.VMEM((width, HD), jnp.bfloat16),
            ],
        ),
        out_shape=[
            jax.ShapeDtypeStruct((tok, HD), out_dtype),
            jax.ShapeDtypeStruct((steps, 1, width), jnp.float32),
            jax.ShapeDtypeStruct((steps, 1, width), jnp.float32),
        ],
        cost_estimate=pl.CostEstimate(flops=4 * 18 * UB * width * HD, bytes_accessed=2 * tok * cols * 2, transcendentals=0),
        compiler_params=pltpu.CompilerParams(dimension_semantics=("arbitrary",), vmem_limit_bytes=VMEM_LIMIT),
        name="value_grads",
    )(low, start, q, g, k)


def attention_keys(low, start, q, g, k, v, top, inv, cos_wide, sin_wide, out_dtype):
    tok, cols = q.shape
    heads = cols // HD
    steps = tok // TB
    width = heads * TB
    return pl.pallas_call(
        functools.partial(key_kernel, heads=heads, scale2=LOG2E / math.sqrt(HD), scale=1.0 / math.sqrt(HD)),
        grid_spec=pltpu.PrefetchScalarGridSpec(
            num_scalar_prefetch=1,
            grid=(steps,),
            in_specs=[
                pl.BlockSpec((1, TB), lambda i, lo: (0, i)),
                pl.BlockSpec((TB, cols), lambda i, lo: (i, 0)),
                pl.BlockSpec((TB, cols), lambda i, lo: (i, 0)),
                pl.BlockSpec((tok, HD), lambda i, lo: (0, 0)),
                pl.BlockSpec((HD, tok), lambda i, lo: (0, 0)),
                pl.BlockSpec((tok, HD), lambda i, lo: (0, 0)),
                pl.BlockSpec((1, 1, width), lambda i, lo: (i, 0, 0)),
                pl.BlockSpec((1, 1, width), lambda i, lo: (i, 0, 0)),
                pl.BlockSpec((tok, HD), lambda i, lo: (0, 0)),
                pl.BlockSpec((tok, HD), lambda i, lo: (0, 0)),
            ],
            out_specs=[
                pl.BlockSpec((tok, HD), lambda i, lo: (0, 0)),
                pl.BlockSpec((TB, cols), lambda i, lo: (i, 0)),
            ],
            scratch_shapes=[
                pltpu.VMEM((tok, width), jnp.float32),
                pltpu.VMEM((tok, width), jnp.float32),
                pltpu.VMEM((tok, HD), jnp.float32),
                pltpu.VMEM((width, HD), jnp.bfloat16),
                pltpu.VMEM((width, HD), jnp.bfloat16),
                pltpu.VMEM((HD, width), jnp.float32),
            ],
        ),
        out_shape=[
            jax.ShapeDtypeStruct((tok, HD), out_dtype),
            jax.ShapeDtypeStruct((tok, cols), jnp.bfloat16),
        ],
        cost_estimate=pl.CostEstimate(flops=8 * 18 * UB * width * HD, bytes_accessed=3 * tok * cols * 2, transcendentals=0),
        compiler_params=pltpu.CompilerParams(dimension_semantics=("arbitrary",), vmem_limit_bytes=VMEM_LIMIT),
        name="key_grads",
    )(low, start, q, g, k, k.T, v, top, inv, cos_wide, sin_wide)


def partial_kernel(order_ref, a_ref, g_ref, drift_ref, out_ref, *, factor):
    grad = dot_nn(a_ref[...], g_ref[...])
    out_ref[0] = (drift_ref[...].astype(jnp.float32) - factor * grad).astype(out_ref.dtype)


def island_partials(order, acts_t, grads, drift, column, factor):
    rows, tok = acts_t.shape
    width = grads.shape[1]
    count = order.shape[0]
    block = rows // count
    base = column // width
    return pl.pallas_call(
        functools.partial(partial_kernel, factor=factor),
        grid_spec=pltpu.PrefetchScalarGridSpec(
            num_scalar_prefetch=1,
            grid=(count,),
            in_specs=[
                pl.BlockSpec((block, tok), lambda s, o: (o[s], 0)),
                pl.BlockSpec((tok, width), lambda s, o: (0, 0)),
                pl.BlockSpec((block, width), lambda s, o: (o[s], base)),
            ],
            out_specs=pl.BlockSpec((1, block, width), lambda s, o: (s, 0, 0)),
        ),
        out_shape=jax.ShapeDtypeStruct((count, block, width), jnp.bfloat16),
        cost_estimate=pl.CostEstimate(
            flops=2 * rows * tok * width, bytes_accessed=2 * (rows * tok + tok * width + 2 * rows * width), transcendentals=0
        ),
        compiler_params=pltpu.CompilerParams(dimension_semantics=("arbitrary",), vmem_limit_bytes=VMEM_LIMIT),
        name="partials",
    )(order, acts_t, grads, drift)


class Ring:
    def __init__(self, count):
        self.count = count
        self.half = count // 2
        self.even = count % 2 == 0
        ring = list(range(0, count, 2)) + list(reversed(range(1, count, 2)))
        self.ups = [(ring[i], ring[(i + 1) % count]) for i in range(count)]
        self.downs = [(ring[i], ring[(i - 1) % count]) for i in range(count)]
        me = lax.axis_index("island")
        self.place = jnp.where(me % 2 == 0, me // 2, count - 1 - me // 2)

    def at(self, offset):
        place = lax.rem(self.place + offset + 2 * self.count, self.count)
        return jnp.where(place < (self.count + 1) // 2, 2 * place, 2 * (self.count - 1 - place) + 1)

    def offsets(self):
        far = [self.half] if self.even else []
        full = range(self.half - 1 if self.even else self.half, 0, -1)
        return far + [sign * s for s in full for sign in (1, -1)] + [0]

    def sum(self, parts):
        offsets = self.offsets()
        width = parts.shape[2]
        halves = (slice(0, width // 2), slice(width // 2, width))
        held = [None, None]
        if self.even:
            held = [
                lax.ppermute(parts[0][:, halves[d]], "island", (self.ups, self.downs)[d]) for d in range(2)
            ]
        at = 1 if self.even else 0
        first = True
        while offsets[at] != 0:
            for d in range(2):
                own = parts[at + d]
                if first and self.even:
                    mine = own[:, halves[d]].astype(jnp.float32) + held[d].astype(jnp.float32)
                    pieces = [mine.astype(jnp.bfloat16), own[:, halves[1 - d]]]
                    own = jnp.concatenate(pieces if d == 0 else pieces[::-1], axis=1)
                elif not first:
                    own = (own.astype(jnp.float32) + held[d].astype(jnp.float32)).astype(jnp.bfloat16)
                held[d] = lax.ppermute(own, "island", (self.ups, self.downs)[d])
            at += 2
            first = False
        own = parts[at].astype(jnp.float32)
        if first and self.even:
            return own + jnp.concatenate(held, axis=1).astype(jnp.float32)
        return own + (held[0].astype(jnp.float32) + held[1].astype(jnp.float32))

    def steps(self, block):
        held = [block, block]
        full = self.half - 1 if self.even else self.half
        for step in range(1, full + 1):
            held = [lax.ppermute(held[d], "island", (self.ups, self.downs)[d]) for d in range(2)]
            yield [(-step, 0, held[0]), (step, 0, held[1])]
        if self.even:
            width = block.shape[1] // 2
            last = [
                lax.ppermute(held[d][:, d * width : (d + 1) * width], "island", (self.ups, self.downs)[d])
                for d in range(2)
            ]
            yield [(-self.half, 0, last[0]), (self.half, width, last[1])]


def fetch_head(columns, mp_count, local_heads):
    rows = columns.shape[0]
    group = QH // KVH
    me = lax.axis_index("mp")

    def pick(device):
        return lax.dynamic_slice_in_dim(columns, device * local_heads // group * HD, HD, 1)

    if mp_count != 4:
        stacked = jnp.stack([pick(j) for j in range(mp_count)])
        return lax.all_to_all(stacked, "mp", split_axis=0, concat_axis=0, tiled=True).reshape(mp_count * rows, HD)
    whole = jnp.zeros((mp_count, rows, HD), columns.dtype)
    got = [pick(me)] + [
        lax.ppermute(pick(me ^ k), "mp", [(i, i ^ k) for i in range(mp_count)]) for k in range(1, mp_count)
    ]
    for k in range(mp_count):
        whole = lax.dynamic_update_index_in_dim(whole, got[k], me ^ k, 0)
    return whole.reshape(mp_count * rows, HD)


def gather_columns(piece, mp_count):
    if mp_count != 4:
        return lax.all_gather(piece, "mp", axis=1, tiled=True)
    me = lax.axis_index("mp")
    far = lax.ppermute(piece, "mp", [(i, i ^ 2) for i in range(mp_count)])
    near = lax.ppermute(piece, "mp", [(i, i ^ 1) for i in range(mp_count)])
    far_near = lax.ppermute(far, "mp", [(i, i ^ 1) for i in range(mp_count)])
    odd = (me & 1) == 1
    upper = (me & 2) == 2
    mine = jnp.where(odd, jnp.concatenate([near, piece], 1), jnp.concatenate([piece, near], 1))
    other = jnp.where(odd, jnp.concatenate([far_near, far], 1), jnp.concatenate([far, far_near], 1))
    return jnp.where(upper, jnp.concatenate([other, mine], 1), jnp.concatenate([mine, other], 1))


def fold_and_gather(piece, mp_count):
    tok = piece.shape[0]
    rows = tok // mp_count
    received = lax.all_to_all(piece.astype(jnp.bfloat16), "mp", split_axis=0, concat_axis=0, tiled=True)
    received = received.astype(jnp.float32).reshape(KVH, mp_count // KVH, rows, HD)
    block = jnp.transpose(jnp.sum(received, axis=1), (1, 0, 2)).reshape(rows, KVH * HD)
    return lax.all_gather(block.astype(jnp.bfloat16), "mp", axis=0, tiled=True)


def body(acts, queries, keys_values, out_grad, segments, drift, outer_weights, momentum):
    tok = acts.shape[1]
    island_count = lax.axis_size("island")
    mp_count = lax.axis_size("mp")
    local_heads = queries.shape[2] // HD
    whole_groups = mp_count == KVH
    half = keys_values.shape[2] // 2
    keys = fetch_head(keys_values[0, :, :half], mp_count, local_heads)
    values = fetch_head(keys_values[0, :, half:], mp_count, local_heads)
    ids = segments[0]
    start = jnp.sum((ids[None, :] < ids[:, None]).astype(jnp.int32), axis=1)
    low = start[::TB] // UB
    start = start[None, :]
    cosine, sine = rope_tables(tok, HD)
    cos_wide = jnp.concatenate([cosine, cosine], axis=1)
    sin_wide = jnp.concatenate([sine, -sine], axis=1)
    acts_t = acts[0].T
    ring = Ring(island_count)
    order = ring.at(jnp.array(ring.offsets(), jnp.int32))
    factor = INNER_LR / math.sqrt(D)

    piece_type = jnp.bfloat16 if whole_groups else jnp.float32
    q, g = queries[0], out_grad[0]
    value_piece, top, inv = attention_values(low, start, q, g, keys, piece_type)
    gather = gather_columns if whole_groups else fold_and_gather
    value_low = gather(value_piece, mp_count)
    key_piece, query_grads = attention_keys(low, start, q, g, keys, values, top, inv, cos_wide, sin_wide, piece_type)
    value_parts = island_partials(order, acts_t, value_low, drift[0], half, factor)
    key_low = gather(key_piece, mp_count)
    key_parts = island_partials(order, acts_t, key_low, drift[0], 0, factor)
    outer, moment, blocks = [], [], []
    for i, parts in enumerate((key_parts, value_parts)):
        cols = slice(i * half, (i + 1) * half)
        outer_grad = -(ring.sum(parts) / island_count)
        new_momentum = MOMENTUM * momentum[0, :, cols] + outer_grad
        new_outer = outer_weights[0, :, cols] - OUTER_LR * (outer_grad + MOMENTUM * new_momentum)
        outer.append(new_outer)
        moment.append(new_momentum)
        blocks.append(new_outer.astype(jnp.bfloat16))
    rows = blocks[0].shape[0]
    gathered = jnp.zeros((island_count, rows, 2 * half), jnp.bfloat16)
    for i in (1, 0):
        gathered = lax.dynamic_update_slice(gathered, blocks[i][None], (ring.at(0), 0, i * half))
    for value_step, key_step in zip(ring.steps(blocks[1]), ring.steps(blocks[0])):
        for i, arrivals in ((1, value_step), (0, key_step)):
            for offset, column, block in arrivals:
                gathered = lax.dynamic_update_slice(gathered, block[None], (ring.at(offset), 0, i * half + column))
    new_outer = jnp.concatenate(outer, axis=1)
    new_momentum = jnp.concatenate(moment, axis=1)
    next_weights = gathered.reshape(island_count * rows, 2 * half)
    return (query_grads[None], new_outer[None], new_momentum[None], next_weights[None])


def solution(mesh):
    in_specs = (
        P("island", None, "mp"),
        P("island", None, "mp"),
        P("island", "mp", None),
        P("island", None, "mp"),
        P("island", None),
        P("island", "mp", None),
        P("mp", "island", None),
        P("mp", "island", None),
    )
    out_specs = (
        P("island", None, "mp"),
        P("mp", "island", None),
        P("mp", "island", None),
        P("mp", None, None),
    )
    return jax.shard_map(body, mesh=mesh, in_specs=in_specs, out_specs=out_specs, check_vma=False)
```
